32 devices in a mesh: space: 8 (over z, y), halo: 4 (over x, core).
Axes of the slice: x: 2, y: 2, z: 4, core: 2. Of those that a mesh axis runs over, the one named last changes fastest.
Arguments:
- positions: float32 [3, 131072], P(None, 'space'), may hold values from -1 to 1
- masses: float32 [131072], P('space'), may hold values from 0.1 to 10
- centres: float32 [4, 3, 128], P('halo'), may hold values from -0.5 to 0.5
- pair_halo: int32 [4, 2048], P('halo', 'space'), may hold values from 0 to 127
- pair_tile: int32 [4, 2048], P('halo', 'space'), may hold values from 0 to 31
- halo_slot: int32 [4, 128], P('halo'), may hold values from 0 to 127, each once within a row
- feedback: float32 [4, 128], P('halo', 'space'), may hold values from 0.5 to 1.5
- mixing: float32 [3, 128, 128], replicated, may hold values from -0.5 to 0.5
- drive: float32 [3, 128], replicated, may hold values from 0.2 to 1
- readout: float32 [3, 128], replicated, may hold values from -1.5 to 1.5
Outputs:
- displacement: float32 [3, 131072], P(None, 'space')
The draws below stay inside these ranges and needn't reach their ends.
All inputs are finite; a program needn't handle non-finite values.
Results may differ from the reference program's by a relative error of at most 0.0003.
Values sent between devices are 32-bit elements; how exact they have to be, the bound alone decides.
No kernel may reach another device: no remote copies, remote signals or barrier semaphores. Data moves between devices by JAX's collectives and lax.ppermute only.
A program may use at most 64 MiB of HBM per device.

```python
import math
import jax
import jax.numpy as jnp
from jax import lax

K = 128
BLK = 512
ITERS = 8
PAIRS_DEV = 256
TILES_DEV = 32
HALOS_PER_GROUP = 128
PAIRS = 2048
PARTICLES = 131072
N_SPACE = 8
N_HALO = 4


def set_ends(result, own_key, smallest, top_value):
    longest = result.shape.index(max(result.shape))
    spots = []
    for shift in (0, 1):
        where = [jax.random.randint(jax.random.fold_in(own_key, axis), (), 0, length) for axis, length in enumerate(result.shape)]
        where[longest] = (where[longest] + shift) % result.shape[longest]
        spots.append(tuple(where))
    return result.at[spots[0]].set(smallest).at[spots[1]].set(top_value)


def level_of(rng, shape, split, smallest, high):
    factor_of, own = 1.0, jax.random.fold_in(rng, 6)
    for axis_at, parts in split:
        draws = jnp.exp(jax.random.uniform(jax.random.fold_in(own, axis_at), (parts,), jnp.float32, smallest / len(split), high / len(split)))
        factor_of = factor_of * jnp.repeat(draws, shape[axis_at] // parts).reshape([-1 if axis == axis_at else 1 for axis in range(len(shape))])
    return factor_of


def gaussian(stream_key, shape, width, most, held_as=jnp.bfloat16):
    result = width * jax.random.normal(stream_key, shape, jnp.float32)
    return jnp.clip(result, min=-most, max=most).astype(held_as)


def setup_inputs(seed: int = 0) -> dict:
    streams_of = jax.random.split(jax.random.key(seed), 11)
    positions = jnp.clip(jax.random.uniform(streams_of[0], (3, PARTICLES), jnp.float32, -1.0, 1.0) * level_of(streams_of[0], (3, PARTICLES), ((1, 8),), -0.4, 0.0), -1.0, 1.0)
    masses = jnp.clip(jnp.exp(math.log(10.0) - 4.6051702 * jax.random.uniform(streams_of[1], (PARTICLES,), jnp.float32) ** level_of(streams_of[1], (PARTICLES,), ((0, 8),), -0.2, 0.2)), 0.1, 10.0)
    centres = jnp.clip(jax.random.uniform(streams_of[2], (N_HALO, 3, HALOS_PER_GROUP), jnp.float32, -0.5, 0.5) * level_of(streams_of[2], (N_HALO, 3, HALOS_PER_GROUP), ((0, 4),), -0.4, 0.0), -0.5, 0.5)
    pair_halo = set_ends(jax.random.randint(streams_of[3], (N_HALO, PAIRS), 0, HALOS_PER_GROUP), jax.random.fold_in(streams_of[3], 1), 0, HALOS_PER_GROUP - 1).astype(jnp.int32)
    pair_tile = set_ends(jax.random.randint(streams_of[4], (N_HALO, PAIRS), 0, TILES_DEV), jax.random.fold_in(streams_of[4], 1), 0, TILES_DEV - 1).astype(jnp.int32)
    halo_slot = jax.vmap(lambda own: jax.random.permutation(own, HALOS_PER_GROUP))(jax.random.split(streams_of[5], N_HALO)).reshape((N_HALO, HALOS_PER_GROUP)).astype(jnp.int32)
    feedback = jnp.clip(0.5 + 1.0 * jax.random.uniform(streams_of[6], (N_HALO, HALOS_PER_GROUP), jnp.float32) ** level_of(streams_of[6], (N_HALO, HALOS_PER_GROUP), ((0, 4), (1, 8)), -0.2, 0.2), 0.5, 1.5)
    mixing = gaussian(streams_of[7], (3, K, K), K ** -0.5, 0.5, jnp.float32)
    drive = jnp.clip(jax.random.uniform(streams_of[8], (3, K), jnp.float32, 0.2, 1.0), 0.2, 1.0)
    readout = gaussian(streams_of[9], (3, K), 0.3, 1.5, jnp.float32)
    return dict(positions=positions, masses=masses, centres=centres, pair_halo=pair_halo, pair_tile=pair_tile, halo_slot=halo_slot, feedback=feedback, mixing=mixing, drive=drive, readout=readout)


def spline_basis(offset, knots):
    radial_distance = jnp.sqrt(lax.optimization_barrier(jnp.sum(offset * offset, axis=0)))
    scaled = radial_distance * ((knots - 1) / 2.6)
    knot_index = jnp.arange(knots, dtype=jnp.float32)
    return jnp.maximum(0.0, 1.0 - jnp.abs(scaled[..., None] - knot_index))

def relax(level, phi, mixing, drive, readout):
    state = jnp.zeros((3,) + level.shape, jnp.float32)
    for relax_iteration in range(ITERS):
        average = lax.optimization_barrier(jnp.mean(state, axis=0))
        fresh = []
        for comp in range(3):
            mixed = jnp.dot(state[comp], mixing[comp], precision=lax.Precision.HIGHEST)
            fresh.append(jnp.tanh(drive[comp] * level + phi[:, None] * mixed + 0.5 * average))
        state = jnp.stack(fresh)
    return lax.optimization_barrier(jnp.sum(state * readout[:, None, :], axis=0))

def reference(positions, masses, centres, pair_halo, pair_tile, halo_slot, feedback, mixing, drive, readout):
    tile_total = TILES_DEV * N_SPACE
    places = positions.reshape(3, tile_total, BLK)
    weights = masses.reshape(tile_total, BLK)
    block = math.gcd(PAIRS, 256)
    total = jnp.zeros((tile_total, 3, BLK), jnp.float32)
    for group in range(N_HALO):
        halo_ids = pair_halo[group]
        owner_space = jnp.arange(PAIRS, dtype=jnp.int32) // PAIRS_DEV
        tile_ids = (owner_space * TILES_DEV + pair_tile[group]).astype(jnp.int32)
        centre_rows = centres[group]

        def project(indices):
            halo_part, tile_part = indices
            offset = places[:, tile_part, :] - centre_rows[:, halo_part][:, :, None]
            basis = spline_basis(offset, K)
            return lax.optimization_barrier(jnp.sum(weights[tile_part][:, :, None] * basis, axis=1))
        pair_rows = lax.map(project, (halo_ids.reshape(-1, block), tile_ids.reshape(-1, block)))
        pair_rows = pair_rows.reshape(PAIRS, K)
        profile = jax.ops.segment_sum(pair_rows, halo_ids, num_segments=HALOS_PER_GROUP)
        level = jnp.log1p(profile)
        phi = feedback[group][halo_slot[group]]
        coef = relax(level, phi, mixing, drive, readout)

        def evaluate(indices):
            halo_part, tile_part = indices
            offset = places[:, tile_part, :] - centre_rows[:, halo_part][:, :, None]
            basis = spline_basis(offset, K)
            scalar = lax.optimization_barrier(jnp.sum(basis * coef[halo_part][:, None, :], axis=2))
            return jnp.transpose(offset * scalar[None], (1, 0, 2))
        shifted_positions = lax.map(evaluate, (halo_ids.reshape(-1, block), tile_ids.reshape(-1, block)))
        shifted_positions = shifted_positions.reshape(PAIRS, 3, BLK)
        total = total + jax.ops.segment_sum(shifted_positions, tile_ids, num_segments=tile_total)
    return jnp.transpose(total, (1, 0, 2)).reshape(3, PARTICLES)
```

```python
import functools

import jax
import jax.numpy as jnp
from jax import lax
from jax.experimental import pallas as pl
from jax.experimental.pallas import tpu as pltpu
from jax.sharding import PartitionSpec as P

BLK = 512
ITERS = 8
LANES = 128
ROWS = 16
F32, BF16 = jnp.float32, jnp.bfloat16


def iota(shape, axis):
    return lax.broadcasted_iota(jnp.int32, shape, axis)


def parts_of(value, count):
    parts = []
    for at in range(count):
        parts.append(value.astype(BF16))
        if at + 1 < count:
            value = value - parts[-1].astype(F32)
    return parts


def bdot(a, b):
    return lax.dot_general(a, b, (((1,), (0,)), ((), ())), preferred_element_type=F32)


def bdot_t(a, b):
    return lax.dot_general(a, b, (((1,), (1,)), ((), ())), preferred_element_type=F32)


def lane_gather(table, index):
    return jnp.take_along_axis(table, index, axis=1, mode="promise_in_bounds")


def pair_centres(cen_ref, halo_row):
    pairs, halos = halo_row.shape[1], cen_ref.shape[2]
    cen = jnp.concatenate([cen_ref[0], jnp.zeros((5, halos), F32)], axis=0)
    blocks = []
    for at in range(pairs // LANES):
        ids = jnp.broadcast_to(halo_row[:, at * LANES : (at + 1) * LANES], (8, LANES))
        found = jnp.zeros((8, LANES), F32)
        for block in range(halos // LANES):
            here = lane_gather(cen[:, block * LANES : (block + 1) * LANES], ids % LANES)
            found = jnp.where(ids // LANES == block, here, found)
        blocks.append(found)
    return jnp.concatenate(blocks, axis=1)


def project_kernel(
    pos_ref, mass_ref, cen_ref, halo_ref, tile_ref, slot_ref, feed_ref,
    out_ref, u_ref, pos_out_ref, m_ref, spread_ref,
):
    pairs, halos = halo_ref.shape[1], slot_ref.shape[1]
    tiles = pos_out_ref.shape[1]
    knots = out_ref.shape[1]
    chunks = BLK // LANES
    for tile in range(tiles):
        block = pos_ref[:, tile * BLK : (tile + 1) * BLK]
        for axis in range(3):
            pos_out_ref[axis, tile : tile + 1, :] = block[axis : axis + 1, :]
    mass = jnp.concatenate(
        [mass_ref[pl.ds(at, tiles, stride=chunks), :] for at in range(chunks)], axis=1
    )
    table = [pos_out_ref[0], pos_out_ref[1], pos_out_ref[2], mass]
    table = jnp.concatenate(
        [jnp.concatenate(three, axis=0) for three in zip(*[parts_of(t, 3) for t in table])]
        if False
        else [jnp.concatenate(parts_of(t, 3), axis=0) for t in table],
        axis=1,
    )
    centre = pair_centres(cen_ref, halo_ref[...])
    row = iota((8, pairs), 0)
    columns = jnp.where(row == 3, jnp.broadcast_to(tile_ref[...], (8, pairs)).astype(F32), centre)
    columns = jnp.transpose(columns)
    tile_of = columns[:, 3:4].astype(jnp.int32)
    lane = iota((pairs, 3 * tiles), 1)
    select = jnp.where(lane % tiles == tile_of, 1.0, 0.0).astype(BF16)
    found = bdot(select, table)
    square = jnp.zeros((pairs, BLK), F32)
    for axis in range(3):
        offset = found[:, axis * BLK : (axis + 1) * BLK] - columns[:, axis : axis + 1]
        square = square + offset * offset
    u_ref[...] = jnp.sqrt(square) * ((knots - 1) / 2.6)
    m_ref[...] = found[:, 3 * BLK :]

    highs = knots // ROWS
    lane = iota((ROWS, LANES), 1)
    sub = iota((ROWS, LANES), 0)
    index = (lane % 8) * ROWS + sub

    def group(at, carry):
        rows = pl.ds(pl.multiple_of(at * ROWS, ROWS), ROWS)
        u = u_ref[rows, :]
        m = m_ref[rows, :]
        whole = jnp.floor(u)
        after = m * (u - whole)
        high = jnp.floor(whole * (1.0 / ROWS))
        low = (whole - high * ROWS).astype(BF16)
        high = high.astype(BF16)
        zero = jnp.zeros(u.shape, BF16)
        one = jnp.ones(u.shape, BF16)
        values = parts_of(m - after, 2) + parts_of(after, 2)
        left = jnp.concatenate(
            [jnp.where(high == h, v, zero) for v in values for h in range(highs)], axis=0
        )
        right = jnp.concatenate([jnp.where(low == b, one, zero) for b in range(ROWS)], axis=0)
        both = bdot_t(left, right)
        for which in range(2):
            spread = jnp.zeros((ROWS, knots), F32)
            for h in range(highs):
                first = ((2 * which) * highs + h) * ROWS
                second = ((2 * which + 1) * highs + h) * ROWS
                tile = both[first : first + ROWS] + both[second : second + ROWS]
                for half in range(2):
                    here = lane_gather(tile[:, half * LANES : (half + 1) * LANES], index)
                    spread = jnp.where(lane // 8 == 2 * h + half, here, spread)
            spread_ref[rows, which * knots : (which + 1) * knots] = spread
        return carry

    lax.fori_loop(0, pairs // ROWS, group, 0)

    owner = jnp.broadcast_to(halo_ref[...], (halos, pairs)) == iota((halos, pairs), 0)
    owner = jnp.where(owner, 1.0, 0.0).astype(BF16)
    total = sum(bdot(owner, part) for part in parts_of(spread_ref[...], 3))
    out_ref[:halos, :] = total[:, :knots] + pltpu.roll(total[:, knots:], 1, 1)

    mine = feed_ref.shape[1]
    slot = slot_ref[...] - lax.axis_index("space") * mine
    phi = jnp.zeros((1, halos), F32)
    for at in range(mine):
        phi = jnp.where(slot == at, feed_ref[0, at], phi)
    out_ref[halos:, :] = jnp.zeros((out_ref.shape[0] - halos, knots), F32)
    for at in range(halos // LANES):
        out_ref[halos + at : halos + at + 1, :] = phi[:, at * LANES : (at + 1) * LANES]


def relax_kernel(
    count, halo_axis, *refs,
):
    profile_refs = refs[:count]
    (
        u_ref, pos_ref, cen_ref, halo_ref, tile_ref, mix_ref, drive_ref, readout_ref,
        keep_ref, send_ref, state_ref, base_ref, weight_ref, table_ref, out_ref,
    ) = refs[count:]
    pairs, halos = halo_ref.shape[1], cen_ref.shape[2]
    tiles, knots = pos_ref.shape[1], drive_ref.shape[1]
    for comp in range(3):
        high, low = parts_of(mix_ref[comp], 2)
        both = jnp.concatenate([high, low], axis=1)
        weight_ref[comp] = jnp.concatenate([both, both], axis=0)
    extra = sum(ref[halos:, :] for ref in profile_refs)
    phi_columns = jnp.transpose(extra)
    for block in range(halos // LANES):
        rows = slice(block * LANES, (block + 1) * LANES)
        level = jnp.log1p(sum(ref[rows, :] for ref in profile_refs))
        phi = phi_columns[:, block : block + 1]
        for comp in range(3):
            base = drive_ref[comp : comp + 1, :] * level
            base_ref[comp] = base
            state_ref[comp] = jnp.tanh(base)

        def step(at, carry):
            old = [state_ref[comp] for comp in range(3)]
            half_mean = (old[0] + old[1] + old[2]) * (0.5 / 3.0)
            for comp in range(3):
                split = jnp.concatenate(parts_of(old[comp], 2), axis=1)
                mixed = bdot(split, weight_ref[comp])
                mixed = mixed[:, :knots] + mixed[:, knots:]
                state_ref[comp] = jnp.tanh(base_ref[comp] + phi * mixed + half_mean)
            return carry

        lax.fori_loop(0, ITERS - 1, step, 0)
        coef = sum(state_ref[comp] * readout_ref[comp : comp + 1, :] for comp in range(3))
        table_ref[rows, :knots] = coef
        table_ref[rows, knots:] = pltpu.roll(coef, knots - 1, 1) - coef

    halo_row, tile_row = halo_ref[...], tile_ref[...]
    halo_column = jnp.transpose(jnp.broadcast_to(halo_row, (8, pairs)).astype(F32))[:, :1]
    owner = jnp.where(halo_column.astype(jnp.int32) == iota((pairs, halos), 1), 1.0, 0.0).astype(BF16)
    tables = sum(bdot(owner, part) for part in parts_of(table_ref[...], 3))
    scalars = []
    for at in range(BLK // LANES):
        u = u_ref[:, at * LANES : (at + 1) * LANES]
        whole = jnp.floor(u)
        index = whole.astype(jnp.int32)
        start = lane_gather(tables[:, :knots], index)
        slope = lane_gather(tables[:, knots:], index)
        scalars.append(start + (u - whole) * slope)
    high, low = parts_of(jnp.concatenate(scalars, axis=1), 2)

    listed = jnp.broadcast_to(tile_row, (tiles, pairs)) == iota((tiles, pairs), 0)
    centre = pair_centres(cen_ref, halo_row)
    left = [jnp.where(listed, 1.0, 0.0).astype(BF16)]
    centre_parts = [part.astype(F32) for part in parts_of(centre, 2)]
    for part in centre_parts:
        for axis in range(3):
            value = jnp.broadcast_to(part[axis : axis + 1, :], (tiles, pairs))
            left.append(jnp.where(listed, value, 0.0).astype(BF16))
    left = jnp.concatenate(left, axis=0)
    from_high = bdot(left, high)
    from_low = bdot(left[: 4 * tiles], low)
    whole = from_high[:tiles] + from_low[:tiles]
    for axis in range(3):
        a, b = (1 + axis) * tiles, (4 + axis) * tiles
        pulled = from_high[a : a + tiles] + from_high[b : b + tiles] + from_low[a : a + tiles]
        out_ref[axis] = pos_ref[axis] * whole - pulled
    half = tiles // 2
    bit = lax.axis_index(halo_axis) % 2
    for ref, which in ((keep_ref, bit), (send_ref, 1 - bit)):
        first = pl.multiple_of(which * half, 8)
        for axis in range(3):
            block = out_ref[axis, pl.ds(first, half), :]
            for at in range(half):
                ref[axis : axis + 1, at * BLK : (at + 1) * BLK] = block[at : at + 1, :]


def butterfly(value, name, size, distance):
    return lax.ppermute(value, name, [(at, at ^ distance) for at in range(size)])


def per_device(
    n_space, n_halo,
    positions, masses, centres, pair_halo, pair_tile, halo_slot, feedback, mixing, drive, readout,
):
    knots = mixing.shape[1]
    particles = masses.shape[0]
    tiles = particles // BLK
    pairs = pair_halo.shape[1]
    halos = halo_slot.shape[1]
    rows = halos + 8 * pl.cdiv(halos // LANES, 8)
    vmem = pl.BlockSpec(memory_space=pltpu.VMEM)
    smem = pl.BlockSpec(memory_space=pltpu.SMEM)
    profile, u, places = pl.pallas_call(
        project_kernel,
        out_shape=(
            jax.ShapeDtypeStruct((rows, knots), F32),
            jax.ShapeDtypeStruct((pairs, BLK), F32),
            jax.ShapeDtypeStruct((3, tiles, BLK), F32),
        ),
        in_specs=[vmem] * 6 + [smem],
        out_specs=(vmem,) * 3,
        scratch_shapes=[pltpu.VMEM((pairs, BLK), F32), pltpu.VMEM((pairs, 2 * knots), F32)],
    )(
        positions, masses.reshape(particles // LANES, LANES), centres,
        pair_halo, pair_tile, halo_slot, feedback,
    )
    held, distance = [profile], 1
    while distance < n_space:
        total = sum(held[1:], held[0])
        if distance == 1 or distance * 2 == n_space:
            steps = [distance]
        else:
            steps = [distance, 2 * distance, 3 * distance]
        held = [total] + [butterfly(total, "space", n_space, step) for step in steps]
        distance *= 2 * len(steps) if len(steps) == 1 else 4
    keep, send = pl.pallas_call(
        functools.partial(relax_kernel, len(held), "halo"),
        out_shape=(jax.ShapeDtypeStruct((3, particles // 2), F32),) * 2,
        in_specs=[vmem] * (len(held) + 8),
        out_specs=(vmem,) * 2,
        scratch_shapes=[
            pltpu.VMEM((3, LANES, knots), F32),
            pltpu.VMEM((3, LANES, knots), F32),
            pltpu.VMEM((3, 2 * knots, 2 * knots), BF16),
            pltpu.VMEM((halos, 2 * knots), F32),
            pltpu.VMEM((3, tiles, BLK), F32),
        ],
    )(*held, u, places, centres, pair_halo, pair_tile, mixing, drive, readout)
    keep = keep + butterfly(send, "halo", n_halo, 1)
    distance = 2
    while distance < n_halo:
        keep = keep + butterfly(keep, "halo", n_halo, distance)
        distance *= 2
    other = butterfly(keep, "halo", n_halo, 1)
    first = lax.axis_index("halo") % 2 == 0
    return jnp.where(
        first, jnp.concatenate([keep, other], axis=1), jnp.concatenate([other, keep], axis=1)
    )


def solution(mesh):
    return jax.shard_map(
        functools.partial(per_device, mesh.shape["space"], mesh.shape["halo"]),
        mesh=mesh,
        in_specs=(
            P(None, "space"),
            P("space"),
            P("halo", None, None),
            P("halo", "space"),
            P("halo", "space"),
            P("halo", None),
            P("halo", "space"),
            P(),
            P(),
            P(),
        ),
        out_specs=P(None, "space"),
        check_vma=False,
    )
```

```python
import functools

import jax
import jax.numpy as jnp
from jax import lax
from jax.experimental import pallas as pl
from jax.experimental.pallas import tpu as pltpu
from jax.sharding import PartitionSpec as P

BLK = 512
ITERS = 8
LANES = 128
PACK = 16
UNROLL = 8
ROOM = 24 << 20
F32, BF16 = jnp.float32, jnp.bfloat16


def iota(shape, axis):
    return lax.broadcasted_iota(jnp.int32, shape, axis)


def parts_of(value, count):
    parts = []
    for at in range(count):
        parts.append(value.astype(BF16))
        if at + 1 < count:
            value = value - parts[-1].astype(F32)
    return parts


def bdot(a, b):
    return lax.dot_general(a, b, (((1,), (0,)), ((), ())), preferred_element_type=F32)


def bdot_t(a, b):
    return lax.dot_general(a, b, (((1,), (1,)), ((), ())), preferred_element_type=F32)


def lane_gather(table, index):
    return jnp.take_along_axis(table, index, axis=1, mode="promise_in_bounds")


def pair_centres(cen_ref, halo_row):
    pairs, halos = halo_row.shape[1], cen_ref.shape[2]
    cen = jnp.concatenate([cen_ref[0], cen_ref[1], cen_ref[2], jnp.zeros((5, halos), F32)], axis=0)
    blocks = []
    for at in range(pairs // LANES):
        ids = jnp.broadcast_to(halo_row[:, at * LANES : (at + 1) * LANES], (8, LANES))
        found = jnp.zeros((8, LANES), F32)
        for block in range(halos // LANES):
            here = lane_gather(cen[:, block * LANES : (block + 1) * LANES], ids & (LANES - 1))
            found = jnp.where((ids >> 7) == block, here, found)
        blocks.append(found)
    return jnp.concatenate(blocks, axis=1)


def project_kernel(
    pos_hbm, mass_hbm, cen_hbm, halo_hbm, tile_hbm, slot_hbm, feed_hbm,
    out_ref, u_ref,
    pos_ref, mass_ref, cen_ref, halo_ref, tile_ref, slot_ref, feed_ref,
    place_ref, m_ref, spread_ref, sems,
):
    sources = (halo_hbm, tile_hbm, cen_hbm, pos_hbm, mass_hbm, slot_hbm, feed_hbm)
    targets = (halo_ref, tile_ref, cen_ref, pos_ref, mass_ref, slot_ref, feed_ref)
    copies = [
        pltpu.make_async_copy(source, target, sems.at[at])
        for at, (source, target) in enumerate(zip(sources, targets))
    ]
    for copy in copies:
        copy.start()
    pairs, halos = halo_ref.shape[1], slot_ref.shape[1]
    tiles = place_ref.shape[1]
    knots = out_ref.shape[1]
    chunks = BLK // LANES
    scale = (knots - 1) / 2.6
    for copy in copies[:3]:
        copy.wait()
    centre = pair_centres(cen_ref, halo_ref[...]) * scale
    select = jnp.broadcast_to(tile_ref[...], (tiles, pairs)) == iota((tiles, pairs), 0)
    select = jnp.where(select, 1.0, 0.0)
    centre = [part.astype(F32) for part in parts_of(centre, 3)]
    pad = jnp.zeros((LANES - 3 * tiles - 24, pairs), F32)
    select = jnp.transpose(jnp.concatenate([select] * 3 + centre + [pad], axis=0)).astype(BF16)
    shape = (LANES - 3 * tiles, 4 * BLK)
    less = (iota(shape, 0) < 24) & ((iota(shape, 0) & 7) == iota(shape, 1) // BLK)
    less = jnp.where(less & (iota(shape, 1) < 3 * BLK), -1.0, 0.0).astype(BF16)
    for copy in copies[3:5]:
        copy.wait()
    for tile in range(tiles):
        block = pos_ref[:, tile * BLK : (tile + 1) * BLK]
        for axis in range(3):
            place_ref[axis, tile : tile + 1, :] = block[axis : axis + 1, :]
    mass = jnp.concatenate(
        [mass_ref[pl.ds(at, tiles, stride=chunks), :] for at in range(chunks)], axis=1
    )
    table = [place_ref[axis] * scale for axis in range(3)] + [mass]
    table = jnp.concatenate([jnp.concatenate(parts_of(t, 3), axis=0) for t in table], axis=1)
    found = bdot(select, jnp.concatenate([table, less], axis=0))
    square = sum(found[:, axis * BLK : (axis + 1) * BLK] ** 2 for axis in range(3))
    u_ref[...] = square * lax.rsqrt(jnp.maximum(square, 1e-30))
    m_ref[...] = found[:, 3 * BLK :]
    for copy in copies[5:]:
        copy.wait()

    lows = 2 * LANES // PACK
    highs = knots // lows
    wide = LANES // PACK
    lane = iota((PACK, LANES), 1)
    index = (lane % wide) * PACK + iota((PACK, LANES), 0)
    window = lane // wide

    def group(at, carry):
        rows = pl.ds(pl.multiple_of(at * PACK, PACK), PACK)
        u = u_ref[rows, :]
        m = m_ref[rows, :]
        whole = jnp.floor(u)
        after = m * (u - whole)
        high = jnp.floor(whole * (1.0 / lows))
        low = (whole - high * lows).astype(BF16)
        high = high.astype(BF16)
        zero = jnp.zeros(u.shape, BF16)
        one = jnp.ones(u.shape, BF16)
        values = parts_of(m - after, 2) + parts_of(after, 2)
        left = jnp.concatenate(
            [jnp.where(high == h, v, zero) for v in values for h in range(highs)], axis=0
        )
        right = jnp.concatenate([jnp.where(low == b, one, zero) for b in range(lows)], axis=0)
        both = bdot_t(left, right)
        for which in range(2):
            spread = jnp.zeros((PACK, knots), F32)
            for h in range(highs):
                first = ((2 * which) * highs + h) * PACK
                other = ((2 * which + 1) * highs + h) * PACK
                tile = both[first : first + PACK] + both[other : other + PACK]
                for half in range(2):
                    here = lane_gather(tile[:, half * LANES : (half + 1) * LANES], index)
                    spread = jnp.where(window == 2 * h + half, here, spread)
            spread_ref[rows, which * knots : (which + 1) * knots] = spread
        return carry

    lax.fori_loop(0, pairs // PACK, group, 0, unroll=UNROLL)

    owner = jnp.broadcast_to(halo_ref[...], (halos, pairs)) == iota((halos, pairs), 0)
    owner = jnp.where(owner, 1.0, 0.0).astype(BF16)
    total = sum(bdot(owner, part) for part in parts_of(spread_ref[...], 2))
    out_ref[:halos, :] = total[:, :knots] + pltpu.roll(total[:, knots:], 1, 1)

    mine = feed_ref.shape[1]
    slot = slot_ref[...] - lax.axis_index("space") * mine
    phi = jnp.zeros((1, halos), F32)
    for at in range(mine):
        phi = jnp.where(slot == at, feed_ref[0, at], phi)
    out_ref[halos:, :] = jnp.zeros((out_ref.shape[0] - halos, knots), F32)
    for at in range(halos // LANES):
        out_ref[halos + at : halos + at + 1, :] = phi[:, at * LANES : (at + 1) * LANES]


def relax_kernel(count, halo_axis, *refs):
    profile_refs = refs[:count]
    (
        u_ref, pos_ref, cen_ref, halo_ref, tile_ref, mix_ref, drive_ref, readout_ref,
        keep_ref, send_ref, state_ref, base_ref, weight_ref, table_ref, sum_ref,
    ) = refs[count:]
    pairs, halos = halo_ref.shape[1], cen_ref.shape[2]
    tiles, knots = pos_ref.shape[1] // BLK, drive_ref.shape[1]
    for comp in range(3):
        high, low = parts_of(mix_ref[comp], 2)
        both = jnp.concatenate([high, low], axis=1)
        weight_ref[comp] = jnp.concatenate([both, both], axis=0)
    extra = sum(ref[halos:, :] for ref in profile_refs)
    phi_columns = jnp.transpose(extra)
    for block in range(halos // LANES):
        rows = slice(block * LANES, (block + 1) * LANES)
        level = jnp.log1p(sum(ref[rows, :] for ref in profile_refs))
        phi = phi_columns[:, block : block + 1]
        for comp in range(3):
            base = drive_ref[comp : comp + 1, :] * level
            base_ref[comp] = base
            state_ref[comp] = jnp.tanh(base)

        def step(at, carry):
            old = [state_ref[comp] for comp in range(3)]
            half_mean = (old[0] + old[1] + old[2]) * (0.5 / 3.0)
            for comp in range(3):
                split = jnp.concatenate(parts_of(old[comp], 2), axis=1)
                mixed = bdot(split, weight_ref[comp])
                mixed = mixed[:, :knots] + mixed[:, knots:]
                state_ref[comp] = jnp.tanh(base_ref[comp] + phi * mixed + half_mean)
            return carry

        lax.fori_loop(0, ITERS - 1, step, 0)
        coef = sum(state_ref[comp] * readout_ref[comp : comp + 1, :] for comp in range(3))
        table_ref[rows, :knots] = coef
        table_ref[rows, knots:] = pltpu.roll(coef, knots - 1, 1) - coef

    halo_row, tile_row = halo_ref[...], tile_ref[...]
    halo_column = jnp.transpose(jnp.broadcast_to(halo_row, (8, pairs)).astype(F32))[:, :1]
    owner = jnp.where(halo_column.astype(jnp.int32) == iota((pairs, halos), 1), 1.0, 0.0).astype(BF16)
    tables = sum(bdot(owner, part) for part in parts_of(table_ref[...], 2))
    centre = pair_centres(cen_ref, halo_row)
    high, low = [part.astype(F32) for part in parts_of(centre, 2)]
    kinds = jnp.concatenate([high[:3], jnp.ones((1, pairs), F32), low[:4]], axis=0)
    tile_row = jnp.broadcast_to(tile_row, (8, pairs))
    left = jnp.concatenate([jnp.where(tile_row == at, kinds, 0.0) for at in range(tiles)], axis=0)
    left = left.astype(BF16)
    for at in range(BLK // LANES):
        u = u_ref[:, at * LANES : (at + 1) * LANES]
        whole = jnp.floor(u)
        index = whole.astype(jnp.int32)
        start = lane_gather(tables[:, :knots], index)
        slope = lane_gather(tables[:, knots:], index)
        high, low = parts_of(start + (u - whole) * slope, 2)
        sum_ref[:, at * LANES : (at + 1) * LANES] = bdot(left, high) + bdot(left, low)
    half = tiles // 2
    bit = lax.axis_index(halo_axis) & 1
    for ref, which in ((keep_ref, bit), (send_ref, 1 - bit)):
        for at in range(half):
            tile = which * half + at
            rows = sum_ref[pl.ds(pl.multiple_of(tile * 8, 8), 8), :]
            pos = pos_ref[:, pl.ds(pl.multiple_of(tile * BLK, BLK), BLK)]
            ref[:, at * BLK : (at + 1) * BLK] = pos * rows[3:4] - rows[:3] - rows[4:7]


def butterfly(value, name, size, distance):
    return lax.ppermute(value, name, [(at, at ^ distance) for at in range(size)])


def per_device(
    n_space, n_halo,
    positions, masses, centres, pair_halo, pair_tile, halo_slot, feedback, mixing, drive, readout,
):
    knots = mixing.shape[1]
    particles = masses.shape[0]
    tiles = particles // BLK
    pairs = pair_halo.shape[1]
    halos = halo_slot.shape[1]
    rows = halos + 8 * pl.cdiv(halos // LANES, 8)
    centres = jnp.transpose(centres, (1, 0, 2))
    room = pltpu.CompilerParams(vmem_limit_bytes=ROOM)
    vmem = pl.BlockSpec(memory_space=pltpu.VMEM)
    hbm = pl.BlockSpec(memory_space=pltpu.HBM)
    profile, u = pl.pallas_call(
        project_kernel,
        out_shape=(
            jax.ShapeDtypeStruct((rows, knots), F32),
            jax.ShapeDtypeStruct((pairs, BLK), F32),
        ),
        in_specs=[hbm] * 7,
        out_specs=(vmem,) * 2,
        scratch_shapes=[
            pltpu.VMEM(positions.shape, F32),
            pltpu.VMEM((particles // LANES, LANES), F32),
            pltpu.VMEM(centres.shape, F32),
            pltpu.VMEM(pair_halo.shape, jnp.int32),
            pltpu.VMEM(pair_tile.shape, jnp.int32),
            pltpu.VMEM(halo_slot.shape, jnp.int32),
            pltpu.SMEM(feedback.shape, F32),
            pltpu.VMEM((3, tiles, BLK), F32),
            pltpu.VMEM((pairs, BLK), F32),
            pltpu.VMEM((pairs, 2 * knots), F32),
            pltpu.SemaphoreType.DMA((7,)),
        ],
        compiler_params=room,
    )(
        *[
            pltpu.with_memory_space_constraint(value, pltpu.HBM)
            for value in (
                positions, masses.reshape(particles // LANES, LANES), centres,
                pair_halo, pair_tile, halo_slot, feedback,
            )
        ]
    )
    held, distance = [profile], 1
    while distance < n_space:
        total = sum(held[1:], held[0])
        if distance == 1 or distance * 2 == n_space:
            steps = [distance]
        else:
            steps = [distance, 2 * distance, 3 * distance]
        held = [total] + [butterfly(total, "space", n_space, step) for step in steps]
        distance *= 2 * len(steps) if len(steps) == 1 else 4
    keep, send = pl.pallas_call(
        functools.partial(relax_kernel, len(held), "halo"),
        out_shape=(jax.ShapeDtypeStruct((3, particles // 2), F32),) * 2,
        in_specs=[vmem] * (len(held) + 8),
        out_specs=(vmem,) * 2,
        scratch_shapes=[
            pltpu.VMEM((3, LANES, knots), F32),
            pltpu.VMEM((3, LANES, knots), F32),
            pltpu.VMEM((3, 2 * knots, 2 * knots), BF16),
            pltpu.VMEM((halos, 2 * knots), F32),
            pltpu.VMEM((8 * tiles, BLK), F32),
        ],
        compiler_params=room,
    )(*held, u, positions, centres, pair_halo, pair_tile, mixing, drive, readout)
    keep = keep + butterfly(send, "halo", n_halo, 1)
    distance = 2
    while distance < n_halo:
        keep = keep + butterfly(keep, "halo", n_halo, distance)
        distance *= 2
    other = butterfly(keep, "halo", n_halo, 1)
    first = lax.axis_index("halo") % 2 == 0
    return jnp.where(
        first, jnp.concatenate([keep, other], axis=1), jnp.concatenate([other, keep], axis=1)
    )


def solution(mesh):
    return jax.shard_map(
        functools.partial(per_device, mesh.shape["space"], mesh.shape["halo"]),
        mesh=mesh,
        in_specs=(
            P(None, "space"),
            P("space"),
            P("halo", None, None),
            P("halo", "space"),
            P("halo", "space"),
            P("halo", None),
            P("halo", "space"),
            P(),
            P(),
            P(),
        ),
        out_specs=P(None, "space"),
        check_vma=False,
    )
```

```python
import functools

import jax
import jax.numpy as jnp
from jax import lax
from jax.experimental import pallas as pl
from jax.experimental.pallas import tpu as pltpu
from jax.sharding import PartitionSpec as P

BLK = 512
ITERS = 8
LANES = 128
PACK = 16
UNROLL = 8
ROOM = 24 << 20
F32, BF16 = jnp.float32, jnp.bfloat16


def iota(shape, axis):
    return lax.broadcasted_iota(jnp.int32, shape, axis)


def parts_of(value, count):
    parts = []
    for at in range(count):
        parts.append(value.astype(BF16))
        if at + 1 < count:
            value = value - parts[-1].astype(F32)
    return parts


def bdot(a, b):
    return lax.dot_general(a, b, (((1,), (0,)), ((), ())), preferred_element_type=F32)


def bdot_t(a, b):
    return lax.dot_general(a, b, (((1,), (1,)), ((), ())), preferred_element_type=F32)


def lane_gather(table, index):
    numbers = lax.GatherDimensionNumbers(
        offset_dims=(),
        collapsed_slice_dims=(1,),
        start_index_map=(1,),
        operand_batching_dims=(0,),
        start_indices_batching_dims=(0,),
    )
    return lax.gather(
        table, index[..., None], numbers, (1, 1),
        mode=lax.GatherScatterMode.PROMISE_IN_BOUNDS,
    )


def pair_centres(cen_ref, halo_row):
    pairs, halos = halo_row.shape[1], cen_ref.shape[2]
    cen = jnp.concatenate([cen_ref[0], cen_ref[1], cen_ref[2], jnp.zeros((5, halos), F32)], axis=0)
    blocks = []
    for at in range(pairs // LANES):
        ids = jnp.broadcast_to(halo_row[:, at * LANES : (at + 1) * LANES], (8, LANES))
        found = jnp.zeros((8, LANES), F32)
        for block in range(halos // LANES):
            here = lane_gather(cen[:, block * LANES : (block + 1) * LANES], ids & (LANES - 1))
            found = jnp.where((ids >> 7) == block, here, found)
        blocks.append(found)
    return jnp.concatenate(blocks, axis=1)


def project_kernel(
    pos_hbm, mass_hbm, cen_hbm, halo_hbm, tile_hbm, slot_hbm, feed_hbm,
    out_ref, u_ref,
    pos_ref, mass_ref, cen_ref, halo_ref, tile_ref, slot_ref, feed_ref,
    place_ref, m_ref, spread_ref, sems,
):
    sources = (halo_hbm, tile_hbm, cen_hbm, pos_hbm, mass_hbm, slot_hbm, feed_hbm)
    targets = (halo_ref, tile_ref, cen_ref, pos_ref, mass_ref, slot_ref, feed_ref)
    copies = [
        pltpu.make_async_copy(source, target, sems.at[at])
        for at, (source, target) in enumerate(zip(sources, targets))
    ]
    for copy in copies:
        copy.start()
    pairs, halos = halo_ref.shape[1], slot_ref.shape[1]
    tiles = place_ref.shape[1]
    knots = out_ref.shape[1]
    chunks = BLK // LANES
    scale = (knots - 1) / 2.6
    for copy in copies[:3]:
        copy.wait()
    centre = pair_centres(cen_ref, halo_ref[...]) * scale
    select = jnp.broadcast_to(tile_ref[...], (tiles, pairs)) == iota((tiles, pairs), 0)
    select = jnp.where(select, 1.0, 0.0)
    centre = [part.astype(F32) for part in parts_of(centre, 3)]
    pad = jnp.zeros((LANES - 3 * tiles - 24, pairs), F32)
    select = jnp.transpose(jnp.concatenate([select] * 3 + centre + [pad], axis=0)).astype(BF16)
    shape = (LANES - 3 * tiles, 4 * BLK)
    less = (iota(shape, 0) < 24) & ((iota(shape, 0) & 7) == iota(shape, 1) // BLK)
    less = jnp.where(less & (iota(shape, 1) < 3 * BLK), -1.0, 0.0).astype(BF16)
    for copy in copies[3:5]:
        copy.wait()
    for tile in range(tiles):
        block = pos_ref[:, tile * BLK : (tile + 1) * BLK]
        for axis in range(3):
            place_ref[axis, tile : tile + 1, :] = block[axis : axis + 1, :]
    mass = jnp.concatenate(
        [mass_ref[pl.ds(at, tiles, stride=chunks), :] for at in range(chunks)], axis=1
    )
    table = [place_ref[axis] * scale for axis in range(3)] + [mass]
    table = jnp.concatenate([jnp.concatenate(parts_of(t, 3), axis=0) for t in table], axis=1)
    found = bdot(select, jnp.concatenate([table, less], axis=0))
    square = sum(found[:, axis * BLK : (axis + 1) * BLK] ** 2 for axis in range(3))
    u_ref[...] = square * lax.rsqrt(jnp.maximum(square, 1e-30))
    m_ref[...] = found[:, 3 * BLK :]
    for copy in copies[5:]:
        copy.wait()

    lows = 2 * LANES // PACK
    highs = knots // lows
    wide = LANES // PACK
    lane = iota((PACK, LANES), 1)
    index = (lane % wide) * PACK + iota((PACK, LANES), 0)
    window = lane // wide

    def group(at, carry):
        rows = pl.ds(pl.multiple_of(at * PACK, PACK), PACK)
        u = u_ref[rows, :]
        m = m_ref[rows, :]
        whole = jnp.floor(u)
        after = m * (u - whole)
        high = jnp.floor(whole * (1.0 / lows))
        low = (whole - high * lows).astype(BF16)
        high = high.astype(BF16)
        zero = jnp.zeros(u.shape, BF16)
        one = jnp.ones(u.shape, BF16)
        values = parts_of(m - after, 2) + parts_of(after, 2)
        left = jnp.concatenate(
            [jnp.where(high == h, v, zero) for v in values for h in range(highs)], axis=0
        )
        right = jnp.concatenate([jnp.where(low == b, one, zero) for b in range(lows)], axis=0)
        both = bdot_t(left, right)
        for which in range(2):
            spread = jnp.zeros((PACK, knots), F32)
            for h in range(highs):
                first = ((2 * which) * highs + h) * PACK
                other = ((2 * which + 1) * highs + h) * PACK
                tile = both[first : first + PACK] + both[other : other + PACK]
                for half in range(2):
                    here = lane_gather(tile[:, half * LANES : (half + 1) * LANES], index)
                    spread = jnp.where(window == 2 * h + half, here, spread)
            spread_ref[rows, which * knots : (which + 1) * knots] = spread
        return carry

    lax.fori_loop(0, pairs // PACK, group, 0, unroll=UNROLL)

    owner = jnp.broadcast_to(halo_ref[...], (halos, pairs)) == iota((halos, pairs), 0)
    owner = jnp.where(owner, 1.0, 0.0).astype(BF16)
    total = sum(bdot(owner, part) for part in parts_of(spread_ref[...], 2))
    out_ref[:halos, :] = total[:, :knots] + pltpu.roll(total[:, knots:], 1, 1)

    mine = feed_ref.shape[1]
    slot = slot_ref[...] - lax.axis_index("space") * mine
    phi = jnp.zeros((1, halos), F32)
    for at in range(mine):
        phi = jnp.where(slot == at, feed_ref[0, at], phi)
    out_ref[halos:, :] = jnp.zeros((out_ref.shape[0] - halos, knots), F32)
    for at in range(halos // LANES):
        out_ref[halos + at : halos + at + 1, :] = phi[:, at * LANES : (at + 1) * LANES]


def prepare_kernel(
    halo_axis, u_ref, cen_ref, halo_ref, tile_ref, mix_ref, drive_ref, readout_ref,
    weight_ref, owner_ref, left_ref, index_ref, part_ref, gains_ref,
):
    pairs, halos = halo_ref.shape[1], cen_ref.shape[2]
    tiles = left_ref.shape[0] // 8
    for comp in range(3):
        high, low = parts_of(mix_ref[comp], 2)
        both = jnp.concatenate([high, low], axis=1)
        weight_ref[comp] = jnp.concatenate([both, both], axis=0)
    halo_row = halo_ref[...]
    halo_column = jnp.transpose(jnp.broadcast_to(halo_row, (8, pairs)).astype(F32))[:, :1]
    owner = halo_column.astype(jnp.int32) == iota((pairs, halos), 1)
    owner_ref[...] = jnp.where(owner, 1.0, 0.0).astype(BF16)
    high, low = [part.astype(F32) for part in parts_of(pair_centres(cen_ref, halo_row), 2)]
    kinds = jnp.concatenate([high[:3], jnp.ones((1, pairs), F32), low[:4]], axis=0)
    first = (lax.axis_index(halo_axis) & 1) * (tiles // 2)
    tile_row = jnp.broadcast_to(tile_ref[...], (8, pairs)) ^ first
    left = jnp.concatenate([jnp.where(tile_row == at, kinds, 0.0) for at in range(tiles)], axis=0)
    left_ref[...] = left.astype(BF16)
    index = u_ref[...].astype(jnp.int32)
    index_ref[...] = index
    part_ref[...] = u_ref[...] - index.astype(F32)
    gains_ref[:3, :] = drive_ref[...]
    gains_ref[3:6, :] = readout_ref[...]
    gains_ref[6:, :] = jnp.zeros_like(gains_ref[6:, :])


def relax_kernel(count, halo_axis, *refs):
    profile_refs = refs[:count]
    (
        weight_ref, owner_ref, left_ref, index_ref, part_ref, gains_ref, pos_ref,
        keep_ref, send_ref, state_ref, base_ref, table_ref,
    ) = refs[count:]
    halos = owner_ref.shape[1]
    tiles, knots = pos_ref.shape[1] // BLK, gains_ref.shape[1]
    extra = sum(ref[halos:, :] for ref in profile_refs)
    phi_columns = jnp.transpose(extra)
    for block in range(halos // LANES):
        rows = slice(block * LANES, (block + 1) * LANES)
        level = jnp.log1p(sum(ref[rows, :] for ref in profile_refs))
        phi = phi_columns[:, block : block + 1]
        for comp in range(3):
            base = gains_ref[comp : comp + 1, :] * level
            base_ref[comp] = base
            state_ref[comp] = jnp.tanh(base)

        def step(at, carry):
            old = [state_ref[comp] for comp in range(3)]
            half_mean = (old[0] + old[1] + old[2]) * (0.5 / 3.0)
            for comp in range(3):
                split = jnp.concatenate(parts_of(old[comp], 2), axis=1)
                mixed = bdot(split, weight_ref[comp])
                mixed = mixed[:, :knots] + mixed[:, knots:]
                state_ref[comp] = jnp.tanh(base_ref[comp] + phi * mixed + half_mean)
            return carry

        lax.fori_loop(0, ITERS - 1, step, 0, unroll=True)
        coef = sum(state_ref[comp] * gains_ref[3 + comp : 4 + comp, :] for comp in range(3))
        table_ref[rows, :knots] = coef
        table_ref[rows, knots:] = pltpu.roll(coef, knots - 1, 1) - coef

    owner = owner_ref[...]
    tables = bdot(
        jnp.concatenate([owner] * 2, axis=1), jnp.concatenate(parts_of(table_ref[...], 2), axis=0)
    )
    left = left_ref[...]
    left = jnp.concatenate([left] * 2, axis=1)
    half = tiles // 2
    first = (lax.axis_index(halo_axis) & 1) * half
    width = 2 * LANES
    for at in range(0, BLK, width):
        scalars = []
        for lanes in (slice(at, at + LANES), slice(at + LANES, at + width)):
            index = index_ref[:, lanes]
            start = lane_gather(tables[:, :knots], index)
            slope = lane_gather(tables[:, knots:], index)
            scalars.append(start + part_ref[:, lanes] * slope)
        sums = bdot(left, jnp.concatenate(parts_of(jnp.concatenate(scalars, axis=1), 2), axis=0))
        for ref, start in ((keep_ref, 0), (send_ref, half)):
            for tile in range(half):
                rows = sums[8 * (start + tile) : 8 * (start + tile + 1)]
                lane = pl.multiple_of(((start + tile) ^ first) * BLK + at, width)
                pos = pos_ref[:, pl.ds(lane, width)]
                ref[:, tile * BLK + at : tile * BLK + at + width] = (
                    pos * rows[3:4] - rows[:3] - rows[4:7]
                )


def butterfly(value, name, size, distance):
    return lax.ppermute(value, name, [(at, at ^ distance) for at in range(size)])


def per_device(
    n_space, n_halo,
    positions, masses, centres, pair_halo, pair_tile, halo_slot, feedback, mixing, drive, readout,
):
    knots = mixing.shape[1]
    particles = masses.shape[0]
    tiles = particles // BLK
    pairs = pair_halo.shape[1]
    halos = halo_slot.shape[1]
    rows = halos + 8 * pl.cdiv(halos // LANES, 8)
    centres = jnp.transpose(centres, (1, 0, 2))
    room = pltpu.CompilerParams(vmem_limit_bytes=ROOM)
    vmem = pl.BlockSpec(memory_space=pltpu.VMEM)
    hbm = pl.BlockSpec(memory_space=pltpu.HBM)
    profile, u = pl.pallas_call(
        project_kernel,
        out_shape=(
            jax.ShapeDtypeStruct((rows, knots), F32),
            jax.ShapeDtypeStruct((pairs, BLK), F32),
        ),
        in_specs=[hbm] * 7,
        out_specs=(vmem,) * 2,
        scratch_shapes=[
            pltpu.VMEM(positions.shape, F32),
            pltpu.VMEM((particles // LANES, LANES), F32),
            pltpu.VMEM(centres.shape, F32),
            pltpu.VMEM(pair_halo.shape, jnp.int32),
            pltpu.VMEM(pair_tile.shape, jnp.int32),
            pltpu.VMEM(halo_slot.shape, jnp.int32),
            pltpu.SMEM(feedback.shape, F32),
            pltpu.VMEM((3, tiles, BLK), F32),
            pltpu.VMEM((pairs, BLK), F32),
            pltpu.VMEM((pairs, 2 * knots), F32),
            pltpu.SemaphoreType.DMA((7,)),
        ],
        compiler_params=room,
    )(
        *[
            pltpu.with_memory_space_constraint(value, pltpu.HBM)
            for value in (
                positions, masses.reshape(particles // LANES, LANES), centres,
                pair_halo, pair_tile, halo_slot, feedback,
            )
        ]
    )
    held, distance = [profile], 1
    while distance < n_space:
        total = sum(held[1:], held[0])
        steps = [3, 2, 1] if 4 * distance <= n_space else [1]
        held = [total] + [butterfly(total, "space", n_space, step * distance) for step in steps]
        distance *= len(steps) + 1
    weight, owner, left, index, part, gains = pl.pallas_call(
        functools.partial(prepare_kernel, "halo"),
        out_shape=(
            jax.ShapeDtypeStruct((3, 2 * knots, 2 * knots), BF16),
            jax.ShapeDtypeStruct((pairs, halos), BF16),
            jax.ShapeDtypeStruct((8 * tiles, pairs), BF16),
            jax.ShapeDtypeStruct((pairs, BLK), jnp.int32),
            jax.ShapeDtypeStruct((pairs, BLK), F32),
            jax.ShapeDtypeStruct((8, knots), F32),
        ),
        in_specs=[vmem] * 7,
        out_specs=(vmem,) * 6,
        compiler_params=room,
        cost_estimate=pl.CostEstimate(flops=0, bytes_accessed=4 << 20, transcendentals=0),
    )(u, centres, pair_halo, pair_tile, mixing, drive, readout)
    keep, send = pl.pallas_call(
        functools.partial(relax_kernel, len(held), "halo"),
        out_shape=(jax.ShapeDtypeStruct((3, particles // 2), F32),) * 2,
        in_specs=[vmem] * (len(held) + 7),
        out_specs=(vmem,) * 2,
        scratch_shapes=[
            pltpu.VMEM((3, LANES, knots), F32),
            pltpu.VMEM((3, LANES, knots), F32),
            pltpu.VMEM((halos, 2 * knots), F32),
        ],
        compiler_params=room,
    )(*held, weight, owner, left, index, part, gains, positions)
    keep = keep + butterfly(send, "halo", n_halo, 1)
    distance = 2
    while distance < n_halo:
        keep = keep + butterfly(keep, "halo", n_halo, distance)
        distance *= 2
    other = butterfly(keep, "halo", n_halo, 1)
    first = lax.axis_index("halo") % 2 == 0
    return jnp.where(
        first, jnp.concatenate([keep, other], axis=1), jnp.concatenate([other, keep], axis=1)
    )


def solution(mesh):
    return jax.shard_map(
        functools.partial(per_device, mesh.shape["space"], mesh.shape["halo"]),
        mesh=mesh,
        in_specs=(
            P(None, "space"),
            P("space"),
            P("halo", None, None),
            P("halo", "space"),
            P("halo", "space"),
            P("halo", None),
            P("halo", "space"),
            P(),
            P(),
            P(),
        ),
        out_specs=P(None, "space"),
        check_vma=False,
    )
```
